256 devices in a mesh: req: 32 (over z_hi, y, core), tp: 8 (over x, z_lo).
Axes of the slice: x: 4, y: 4, z: 8 (z_hi: 4, z_lo: 2; z = z_hi * 2 + z_lo), core: 2. Of those that a mesh axis runs over, the one named last changes fastest.
Arguments:
- suffix: bfloat16 [256, 64, 2048], P('tp', 'req')
- prefix_store: bfloat16 [32, 2048, 2, 2048], P('req', None, None, 'tp')
- prefix_owner: int32 [2], replicated, may hold values from 0 to 31, as said below
- prefix_group: int32 [64], replicated, may hold values from 0 to 1
- request_perm: int32 [64], replicated, may hold values from 0 to 63, each once
- suffix_len: int32 [64], replicated, may hold values from 1 to 256, 8192 in all
- ln_gain_attn: float32 [2048], replicated, may hold values from 0.1 to 1.9
- w_qkv: bfloat16 [2048, 3, 2048], P(None, None, 'tp'), may hold values from -0.125 to 0.125
- w_out_attn: bfloat16 [2048, 2048], P('tp'), may hold values from -2.390625 to 2.390625
- ln_gain_mlp: float32 [2048], replicated, may hold values from 0.1 to 1.9
- w_in: bfloat16 [2048, 5120], P(None, 'tp'), may hold values from -0.125 to 0.125
- w_down: bfloat16 [5120, 2048], P('tp'), may hold values from -0.078125 to 0.078125
Outputs:
- layer_out: bfloat16 [256, 64, 2048], P('tp', 'req')
The draws below stay inside these ranges and needn't reach their ends.
Inputs may be any that keep to these rules, and one draw needn't show every extreme that they name: `prefix_owner`: 2 different block indices. `request_perm`: each request exactly once.
All inputs are finite; a program needn't handle non-finite values.
Results may differ from the reference program's by a relative error of at most 0.015.
The reference program's roundings to bfloat16 on the way (of `cache`, `normed`, `projected`, `weights`, `context`, `hidden`, `normed_mlp` and `inner`) count: a program that leaves them out, or rounds other values in their place, can miss the bound.
Values may be sent and summed in bfloat16 or wider, within the bound.
A program may use at most 64 MiB of HBM per device.

```python
import math
import jax
import jax.numpy as jnp
import numpy as np
from jax import lax

D = 2048
H = 16
HD = 128
FFW = 5120
SLOT = 256
PL = 2048
G = 2
REQS = 64
N_REQ = 32
N_TP = 8


def draw_suffix(key, part):
    first, second, third = jax.random.split(key, 3)
    row_scale = jnp.exp(jax.random.uniform(second, (SLOT, REQS, 1), jnp.float32, math.log(0.5), math.log(2.0)))
    column_scale = jnp.exp(jax.random.uniform(third, (1, 1, D), jnp.float32, math.log(0.5), math.log(2.0)))
    base = jax.random.normal(first, (SLOT, REQS, D), jnp.float32)
    return (base * row_scale * column_scale).astype(jnp.bfloat16)


def draw_prefix_store(key, part):
    first = jax.random.fold_in(key, 0)
    base = jax.random.normal(first, (N_REQ, PL, 2, D), jnp.float32)
    return base.astype(jnp.bfloat16)


def draw_prefix_owner(key, part):
    first, second = jax.random.split(key, 2)
    others = jax.random.permutation(first, N_REQ - 1)[:G].astype(jnp.int32)
    chosen = jax.random.randint(second, (), 0, G)
    return jnp.where(jnp.arange(G) == chosen, N_REQ - 1, others).astype(jnp.int32)


def touch_ends(values, stream_key, low, largest):
    longest = values.shape.index(max(values.shape))
    spots = []
    for shift in (0, 1):
        where = [jax.random.randint(jax.random.fold_in(stream_key, axis), (), 0, length) for axis, length in enumerate(values.shape)]
        where[longest] = (where[longest] + shift) % values.shape[longest]
        spots.append(tuple(where))
    return values.at[spots[0]].set(low).at[spots[1]].set(largest)


def level_of(stream_key, dims, pieces, smallest, largest):
    def one(axis_at, shards_of):
        heights = jax.random.uniform(jax.random.fold_in(jax.random.fold_in(stream_key, 6), axis_at), (shards_of,), jnp.float32, smallest / len(pieces), largest / len(pieces))
        return jnp.repeat(jnp.exp(heights), dims[axis_at] // shards_of).reshape((-1,) + (1,) * (len(dims) - axis_at - 1))

    factor_of = one(*pieces[0])
    for cut in pieces[1:]:
        factor_of = factor_of * one(*cut)
    return factor_of


def length_profile(amount, total, reach, skew):
    weights = [(1 << 20) // math.isqrt(rank ** skew) + 1 for rank in range(2, amount + 1)]
    surplus, given = total - reach - (amount - 1), [1] * (amount - 1)
    while surplus > 0:
        movable = [i for i in range(amount - 1) if given[i] < reach]
        mass, left = sum([weights[i] for i in movable]), surplus
        for i in movable:
            addition = min(reach - given[i], max(1, left * weights[i] // mass), surplus)
            given[i] = given[i] + addition
            surplus = surplus - addition
    return np.array([reach] + given)


def uneven(own_key, number_of, total, reach, slope):
    if number_of == 2:
        one = jax.random.randint(own_key, (), max(1, total - reach), min(reach, total - 1) + 1)
        return jnp.stack([one, total - one])
    lengths = jnp.asarray(length_profile(number_of, total, reach, slope), jnp.int32)
    couples = (number_of - 1) // 2
    giver, taker = lengths[1:1 + 2 * couples:2], lengths[2:2 + 2 * couples:2]
    margin = jnp.minimum(giver - 1, reach - taker)
    passed = jax.random.randint(jax.random.fold_in(own_key, 1), (couples,), 0, 1 << 20) % (margin + 1)
    lengths = lengths.at[1:1 + 2 * couples:2].set(giver - passed).at[2:2 + 2 * couples:2].set(taker + passed)
    return lengths[jax.random.permutation(jax.random.fold_in(own_key, 2), number_of)]


def normal_values(stream_key, shape, deviation, most, shards=(), held_as=jnp.bfloat16):
    level = level_of(stream_key, shape, shards, -0.22, 0.18) if shards else 1.0
    values = jax.random.normal(stream_key, shape, jnp.float32) * deviation * level
    return jnp.minimum(jnp.maximum(values, -most), most).astype(held_as)


def setup_inputs(seed: int = 0) -> dict:
    streams_of = jax.random.split(jax.random.key(seed), 13)
    return {
        "suffix": draw_suffix(jax.random.fold_in(streams_of[12], 71), 0),
        "prefix_store": draw_prefix_store(jax.random.fold_in(streams_of[12], 71), 0),
        "prefix_owner": draw_prefix_owner(jax.random.fold_in(streams_of[12], 71), 0),
        "prefix_group": touch_ends(jax.random.randint(streams_of[3], (REQS,), 0, G), jax.random.fold_in(streams_of[3], 1), 0, G - 1).astype(jnp.int32),
        "request_perm": jax.random.permutation(streams_of[4], REQS).astype(jnp.int32),
        "suffix_len": uneven(streams_of[5], REQS, REQS * SLOT // 2, SLOT, 2).astype(jnp.int32),
        "ln_gain_attn": jnp.clip(1.0 + 0.18 * jax.random.normal(streams_of[6], (D,), jnp.float32), 0.1, 1.9),
        "w_qkv": normal_values(streams_of[7], (D, 3, D), D ** -0.5, 0.125, ((2, 8),)),
        "w_out_attn": normal_values(streams_of[8], (D, D), 0.4, 2.390625, ((0, 8),)),
        "ln_gain_mlp": jnp.clip(1.0 + 0.18 * jax.random.normal(streams_of[9], (D,), jnp.float32), 0.1, 1.9),
        "w_in": normal_values(streams_of[10], (D, FFW), D ** -0.5, 0.125, ((1, 8),)),
        "w_down": normal_values(streams_of[11], (FFW, D), FFW ** -0.5, 0.078125, ((0, 8),)),
    }


def layer_norm(values, gain):
    values = values.astype(jnp.float32)
    center = values - lax.optimization_barrier(jnp.mean(values, -1, keepdims=True))
    spread = lax.optimization_barrier(jnp.mean(center * center, -1, keepdims=True))
    return center * lax.rsqrt(spread + 1e-05) * gain

def grouped_sum(left, right, groups):
    rows = left.shape[0]
    inner_width = left.shape[1] // groups
    left_parts = left.astype(jnp.float32).reshape(rows, groups, inner_width)
    right_parts = right.reshape(groups, inner_width, right.shape[1])
    parts = jnp.einsum('sgk,gkd->gsd', left_parts, right_parts).astype(jnp.bfloat16)
    parts = lax.optimization_barrier(parts)
    return lax.optimization_barrier(jnp.sum(parts.astype(jnp.float32), 0))

def reference(suffix, prefix_store, prefix_owner, prefix_group, request_perm, suffix_len, ln_gain_attn, w_qkv, w_out_attn, ln_gain_mlp, w_in, w_down):
    scale = HD ** (-0.5)
    places = jnp.arange(SLOT, dtype=jnp.int32)
    flat_qkv = w_qkv.reshape(D, 3 * D)
    out_wide = w_out_attn.astype(jnp.float32)
    down_wide = w_down.astype(jnp.float32)

    def one_slot(slot):
        request = request_perm[slot]
        length = suffix_len[request]
        owner = prefix_owner[prefix_group[request]]
        rows = lax.dynamic_index_in_dim(suffix, slot, 1, keepdims=False)
        normed = layer_norm(rows, ln_gain_attn).astype(jnp.bfloat16)
        projected = jnp.dot(normed, flat_qkv, preferred_element_type=jnp.float32).astype(jnp.bfloat16)
        projected = projected.reshape(SLOT, 3, H, HD)
        cache = lax.dynamic_index_in_dim(prefix_store, owner, 0, keepdims=False)
        keys_all = jnp.concatenate([cache[:, 0].reshape(PL, H, HD), projected[:, 1]], 0)
        values_all = jnp.concatenate([cache[:, 1].reshape(PL, H, HD), projected[:, 2]], 0)
        scores = jnp.einsum('shd,thd->hst', projected[:, 0].astype(jnp.float32), keys_all.astype(jnp.float32)) * scale
        own_visible = (places[None, :] <= places[:, None]) & (places[None, :] < length)
        visible = jnp.concatenate([jnp.ones((SLOT, PL), bool), own_visible], 1)
        scores = jnp.where(visible[None], scores, -jnp.inf)
        highest = lax.optimization_barrier(jnp.max(scores, -1, keepdims=True))
        raised = jnp.exp(scores - highest)
        weights = (raised / lax.optimization_barrier(jnp.sum(raised, -1, keepdims=True))).astype(jnp.bfloat16)
        context = jnp.einsum('hst,thd->shd', weights.astype(jnp.float32), values_all.astype(jnp.float32))
        context = context.reshape(SLOT, D).astype(jnp.bfloat16)
        attention = grouped_sum(context, out_wide, N_TP)
        hidden = (rows.astype(jnp.float32) + attention).astype(jnp.bfloat16)
        normed_mlp = layer_norm(hidden, ln_gain_mlp).astype(jnp.bfloat16)
        inner = jax.nn.gelu(jnp.dot(normed_mlp, w_in, preferred_element_type=jnp.float32), approximate=False).astype(jnp.bfloat16)
        down = grouped_sum(inner, down_wide, N_TP)
        valid = (places < length)[:, None]
        return jnp.where(valid, hidden.astype(jnp.float32) + down, 0.0).astype(jnp.bfloat16)
    result = lax.map(one_slot, jnp.arange(REQS, dtype=jnp.int32))
    return jnp.transpose(result, (1, 0, 2))
```

```python
import functools

import jax
import jax.numpy as jnp
from jax import lax
from jax.experimental import pallas as pl
from jax.experimental.pallas import tpu as pltpu
from jax.sharding import PartitionSpec as P

HD = 128
MESH = pl.DeviceIdType.MESH
F32 = jnp.float32
BF16 = jnp.bfloat16
VMEM_LIMIT = 60 * 1024 * 1024


class Place:
    def __init__(self):
        r, t = lax.axis_index("req"), lax.axis_index("tp")
        self.r, self.t = r, t
        self.core, self.y, self.zh = r % 2, (r // 2) % 4, r // 8
        self.x, self.zl = t // 2, t % 2
        self.mate = {"req": r + 1 - 2 * self.core}
        self.yp = {"req": self.zh * 8 + ((self.y + 1) % 4) * 2 + self.core}
        self.ym = {"req": self.zh * 8 + ((self.y + 3) % 4) * 2 + self.core}
        self.zp = {"req": ((self.zh + 1) % 4) * 8 + self.y * 2 + self.core}
        self.zm = {"req": ((self.zh + 3) % 4) * 8 + self.y * 2 + self.core}
        self.xp = {"tp": ((self.x + 1) % 4) * 2 + self.zl}
        self.xm = {"tp": ((self.x + 3) % 4) * 2 + self.zl}
        self.zz = {"tp": self.x * 2 + 1 - self.zl}


class Wire:
    def __init__(self, ssem, rsem):
        self.ssem, self.rsem, self.n, self.sent = ssem, rsem, 0, []

    def send(self, src, dst, to, into=None):
        k = self.n
        self.n += 1
        copy = pltpu.make_async_remote_copy(
            src_ref=src, dst_ref=dst, send_sem=self.ssem.at[k], recv_sem=self.rsem.at[k],
            device_id=to, device_id_type=MESH)
        copy.start()
        self.sent.append(copy)
        into = dst if into is None else into
        here = pltpu.make_async_remote_copy(
            src_ref=into, dst_ref=into, send_sem=self.ssem.at[k], recv_sem=self.rsem.at[k],
            device_id=to, device_id_type=MESH)
        return here.wait_recv

    def drain(self):
        for copy in self.sent:
            copy.wait_send()


def greet(peers):
    barrier = pltpu.get_barrier_semaphore()
    for peer in peers:
        pl.semaphore_signal(barrier, inc=1, device_id=peer, device_id_type=MESH)
    pl.semaphore_wait(barrier, len(peers))


def merge(streams):
    due = [next(s, None) for s in streams]
    while any(d is not None for d in due):
        i = min((d, k) for k, d in enumerate(due) if d is not None)[1]
        due[i] = next(streams[i], None)


def scatter_ring(wire, at, me, left, right, rooms, mix, final, times):
    rbr, rbl, fr, fl = rooms
    opp, nxt, prv = (me + 2) % 4, (me + 1) % 4, (me + 3) % 4
    w_rbr = wire.send(at(opp, 0), rbr, left)
    w_rbl = wire.send(at(opp, 1), rbl, right)
    w_fr1 = wire.send(at(prv, 1), fr.at[1], left)
    w_fl0 = wire.send(at(nxt, 0), fl.at[0], right)
    yield times[0]
    w_rbr()
    mix(at(prv, 0), rbr)
    w_fr0 = wire.send(at(prv, 0), fr.at[0], left)
    w_rbl()
    mix(at(nxt, 1), rbl)
    w_fl1 = wire.send(at(nxt, 1), fl.at[1], right)
    yield times[1]
    w_fr1()
    w_fl0()
    w_fr0()
    w_fl1()
    for j in range(2):
        final(j, at(me, j), fr.at[j], fl.at[j])


def gather_ring(wire, at, me, left, right, times, got=None):
    opp, nxt, prv = (me + 2) % 4, (me + 1) % 4, (me + 3) % 4
    w_r = wire.send(at(me, None), at(me, None), left, at(nxt, None))
    w_l = wire.send(at(me, None), at(me, None), right, at(prv, None))
    yield times[0]
    w_l()
    w_o0 = wire.send(at(prv, 0), at(prv, 0), right, at(opp, 0))
    if got:
        got(prv)
    w_r()
    w_o1 = wire.send(at(nxt, 1), at(nxt, 1), left, at(opp, 1))
    if got:
        got(nxt)
    yield times[1]
    w_o0()
    w_o1()
    if got:
        got(opp)


def rows_at(ref, base, size):
    def at(k, j):
        if j is None:
            return ref.at[pl.ds(pl.multiple_of(base + k * size, size), size)]
        half = size // 2
        return ref.at[pl.ds(pl.multiple_of(base + k * size + j * half, half), half)]

    return at


def normalize(values, gain):
    values = values.astype(F32)
    center = values - jnp.mean(values, -1, keepdims=True)
    spread = jnp.mean(center * center, -1, keepdims=True)
    return (center * lax.rsqrt(spread + 1e-05) * gain).astype(BF16)


def gather_z_first(wire, p, ref, times):
    own = ref.at[pl.ds(pl.multiple_of(p.t * 32, 32), 32)]
    w_z = wire.send(own, own, p.zz, ref.at[pl.ds(pl.multiple_of(p.x * 64 + (1 - p.zl) * 32, 32), 32)])

    def at(zl):
        def inner(k, j):
            if j is None:
                return ref.at[pl.ds(pl.multiple_of(k * 64 + zl * 32, 32), 32)]
            return ref.at[pl.ds(pl.multiple_of(k * 64 + zl * 32 + j * 16, 16), 16)]
        return inner

    mine = gather_ring(wire, at(p.zl), p.x, p.xm, p.xp, times[1:3])
    next(mine)
    yield times[0]
    w_z()
    other = gather_ring(wire, at(1 - p.zl), p.x, p.xm, p.xp, times[3:5])
    next(other)
    yield times[1]
    next(mine)
    yield times[2]
    next(mine, None)
    yield times[3]
    next(other)
    yield times[4]
    next(other, None)


def gather_x_first(wire, p, ref, times):
    def piece(k, zl):
        return ref.at[pl.ds(pl.multiple_of(k * 64 + zl * 32, 32), 32)]

    def at(k, j):
        if j is None:
            return piece(k, p.zl)
        return ref.at[pl.ds(pl.multiple_of(k * 64 + p.zl * 32 + j * 16, 16), 16)]

    waits = []

    def got(k):
        waits.append(wire.send(piece(k, p.zl), piece(k, p.zl), p.zz, piece(k, 1 - p.zl)))

    ring = gather_ring(wire, at, p.x, p.xm, p.xp, times[0:2], got)
    due = next(ring)
    got(p.x)
    while due is not None:
        yield due
        due = next(ring, None)
    yield times[2]
    for wait in waits:
        wait()


def prefix_half(wire, p, a, kv, own, par, rooms, owner, times):
    held = owner == p.r
    chip = owner // 2 == p.r // 2
    row = owner // 8 == p.zh
    con, done = own.at[a], kv.at[p.core, a]
    con[...] = jnp.where(held, own[a], par[a])
    yrooms, zrooms = rooms
    whose = {}

    def mix(ref, got):
        ref[...] = jnp.where(whose["own"], ref[...], got[...])

    def final(j, ref, fr, fl):
        d = (whose["at"] - whose["me"] + 4) % 4
        far = fr if j == 0 else fl
        near, near_d = (fl, 3) if j == 0 else (fr, 1)
        into = whose["into"](whose["me"], j)
        into[...] = jnp.where(d == 0, ref[...], jnp.where(d == near_d, near[...], far[...]))

    yat = rows_at(con, 0, 512)
    whose.update(own=chip, at=(owner // 2) % 4, me=p.y, into=yat)
    yield from scatter_ring(wire, yat, p.y, p.ym, p.yp, yrooms, mix, final, times[0:2])
    zat, zdone = rows_at(con, p.y * 512, 128), rows_at(done, p.y * 512, 128)
    ydone = rows_at(done, 0, 512)
    whose.update(own=row, at=owner // 8, me=p.zh, into=zdone)
    yield from scatter_ring(wire, zat, p.zh, p.zm, p.zp, zrooms, mix, final, times[2:4])
    yield from gather_ring(wire, zdone, p.zh, p.zm, p.zp, times[4:6])
    theirs = rows_at(kv.at[1 - p.core, a], 0, 512)
    waits = []

    def got(k):
        waits.append(wire.send(ydone(k, None), ydone(k, None), p.mate, theirs(k, None)))

    ring = gather_ring(wire, ydone, p.y, p.ym, p.yp, times[6:8], got)
    due = next(ring)
    got(p.y)
    while due is not None:
        yield due
        due = next(ring, None)
    yield times[8]
    for wait in waits:
        wait()


def attend(qkv, kv, ctx, s, group, length):
    scale = HD ** (-0.5)
    rows = lax.broadcasted_iota(jnp.int32, (256, 256), 0)
    cols = lax.broadcasted_iota(jnp.int32, (256, 256), 1)
    visible = (cols <= rows) & (cols < length)
    nt = (((1,), (1,)), ((), ()))
    for h in range(2):
        lanes = slice(h * HD, (h + 1) * HD)
        q = qkv[0, s, :, lanes]
        pre = lax.dot_general(q, kv[group, 0, :, lanes], nt, preferred_element_type=F32) * scale
        own = lax.dot_general(q, qkv[1, s, :, lanes], nt, preferred_element_type=F32) * scale
        own = jnp.where(visible, own, -jnp.inf)
        top = jnp.maximum(jnp.max(pre, -1, keepdims=True), jnp.max(own, -1, keepdims=True))
        pre = jnp.exp(pre - top)
        own = jnp.exp(own - top)
        total = jnp.sum(pre, -1, keepdims=True) + jnp.sum(own, -1, keepdims=True)
        out = jnp.dot(pre.astype(BF16), kv[group, 1, :, lanes], preferred_element_type=F32)
        out = out + jnp.dot(own.astype(BF16), qkv[2, s, :, lanes], preferred_element_type=F32)
        ctx[s, :, lanes] = (out / total).astype(BF16)


def first_kernel(owner_ref, group_ref, perm_ref, len_ref, x_ref, gain_ref, block, w_any, ctx,
                 xg, own, par, kv, w, qkv, yr0, yf0, yr1, yf1, zr0, zf0, zr1, zf1, ssem, rsem, lsem):
    p = Place()
    copies = [pltpu.make_async_copy(block.at[a], own.at[a], lsem.at[a]) for a in range(2)]
    weights = pltpu.make_async_copy(w_any, w, lsem.at[2])
    for copy in copies:
        copy.start()
    weights.start()
    greet([p.mate, p.yp, p.ym, p.zp, p.zm, p.xp, p.xm, p.zz])
    wire = Wire(ssem, rsem)
    w_par = [wire.send(block.at[a], par.at[a], p.mate) for a in range(2)]
    for s in range(2):
        xg[s, pl.ds(pl.multiple_of(p.t * 32, 32), 32)] = normalize(x_ref[s], gain_ref[...])
    owner = owner_ref[p.core]

    def prefix(a, start, times):
        yield start
        copies[a].wait()
        w_par[a]()
        yr, yf, zr, zf = ((yr0, yf0, zr0, zf0), (yr1, yf1, zr1, zf1))[a]
        rooms = ((yr.at[0], yr.at[1], yf.at[0], yf.at[1]), (zr.at[0], zr.at[1], zf.at[0], zf.at[1]))
        yield from prefix_half(wire, p, a, kv, own, par, rooms, owner, times)

    def project(start):
        yield start
        weights.wait()
        for s in (1, 0):
            @pl.loop(0, 3)
            def _(j):
                qkv[j, s] = jnp.dot(xg[s], w[j], preferred_element_type=F32).astype(BF16)
            yield start + 1

    merge([
        gather_z_first(wire, p, xg.at[0], (4, 9, 12, 15, 18)),
        gather_x_first(wire, p, xg.at[1], (5, 8, 20)),
        prefix(0, 2, (8, 12, 15, 18, 21, 24, 29, 33, 40)),
        prefix(1, 5, (15, 20, 24, 26, 29, 31, 38, 42, 46)),
        project(21),
    ])
    for s in range(2):
        request = perm_ref[p.r * 2 + s]
        attend(qkv, kv, ctx, s, group_ref[request], len_ref[request])
    wire.drain()


def add_rings(wire, p, part, rooms, times):
    pass


def gelu(v):
    return jax.nn.gelu(v, approximate=False)


def on_device(suffix, prefix_store, prefix_owner, prefix_group, request_perm, suffix_len, ln_gain_attn,
              w_qkv, w_out_attn, ln_gain_mlp, w_in, w_down):
    rows = jnp.transpose(suffix, (1, 0, 2))
    block = jnp.transpose(prefix_store[0], (1, 0, 2))
    w3 = jnp.transpose(w_qkv, (1, 0, 2))
    vm = pl.BlockSpec(memory_space=pltpu.VMEM)
    sm = pl.BlockSpec(memory_space=pltpu.SMEM)
    anym = pl.BlockSpec(memory_space=pl.ANY)
    context = pl.pallas_call(
        first_kernel,
        out_shape=jax.ShapeDtypeStruct((2, 256, 256), BF16),
        in_specs=[sm, sm, sm, sm, vm, vm, anym, anym],
        out_specs=vm,
        scratch_shapes=[
            pltpu.VMEM((2, 256, 2048), BF16),
            pltpu.VMEM((2, 2048, 256), BF16),
            pltpu.VMEM((2, 2048, 256), BF16),
            pltpu.VMEM((2, 2, 2048, 256), BF16),
            pltpu.VMEM((3, 2048, 256), BF16),
            pltpu.VMEM((3, 2, 256, 256), BF16),
            pltpu.VMEM((2, 256, 256), BF16),
            pltpu.VMEM((2, 2, 256, 256), BF16),
            pltpu.VMEM((2, 256, 256), BF16),
            pltpu.VMEM((2, 2, 256, 256), BF16),
            pltpu.VMEM((2, 64, 256), BF16),
            pltpu.VMEM((2, 2, 64, 256), BF16),
            pltpu.VMEM((2, 64, 256), BF16),
            pltpu.VMEM((2, 2, 64, 256), BF16),
            pltpu.SemaphoreType.DMA((96,)),
            pltpu.SemaphoreType.DMA((96,)),
            pltpu.SemaphoreType.DMA((4,)),
        ],
        compiler_params=pltpu.CompilerParams(
            collective_id=0, has_side_effects=True, vmem_limit_bytes=VMEM_LIMIT),
        name="gather_project_attend",
    )(prefix_owner, prefix_group, request_perm, suffix_len, rows, ln_gain_attn.reshape(1, -1), block, w3)
    context = jnp.transpose(context, (1, 0, 2))
    return rest(context, suffix, request_perm, suffix_len, w_out_attn, ln_gain_mlp, w_in, w_down)


def layer_norm(values, gain):
    values = values.astype(jnp.float32)
    center = values - jnp.mean(values, -1, keepdims=True)
    spread = jnp.mean(center * center, -1, keepdims=True)
    return center * lax.rsqrt(spread + 1e-05) * gain


def rest(context, suffix, request_perm, suffix_len, w_out_attn, ln_gain_mlp, w_in, w_down):
    part_rows, slots_dev, _ = suffix.shape
    slots = lax.axis_index("req") * slots_dev + jnp.arange(slots_dev, dtype=jnp.int32)
    lengths = jnp.take(suffix_len, jnp.take(request_perm, slots))
    first_row = lax.axis_index("tp") * part_rows
    attention = lax.psum_scatter(
        jnp.einsum("srk,kd->srd", context, w_out_attn, preferred_element_type=jnp.float32).astype(
            jnp.bfloat16), "tp", scatter_dimension=0, tiled=True).astype(jnp.float32)
    hidden = (suffix.astype(jnp.float32) + attention).astype(jnp.bfloat16)
    normed = layer_norm(hidden, ln_gain_mlp).astype(jnp.bfloat16)
    product = jnp.einsum("srd,df->srf", lax.all_gather(normed, "tp", axis=0, tiled=True), w_in,
                         preferred_element_type=jnp.float32)
    inner = jax.nn.gelu(product, approximate=False).astype(jnp.bfloat16)
    down = lax.psum_scatter(
        jnp.einsum("srf,fd->srd", inner, w_down, preferred_element_type=jnp.float32).astype(
            jnp.bfloat16), "tp", scatter_dimension=0, tiled=True).astype(jnp.float32)
    places = first_row + jnp.arange(part_rows, dtype=jnp.int32)
    valid = places[:, None] < lengths[None, :]
    return jnp.where(valid[:, :, None], hidden.astype(jnp.float32) + down, 0.0).astype(jnp.bfloat16)


def solution(mesh):
    placed = (P("tp", "req", None), P("req", None, None, "tp"), P(), P(), P(), P(), P(),
              P(None, None, "tp"), P("tp", None), P(), P(None, "tp"), P("tp", None))
    return jax.shard_map(
        on_device, mesh=mesh, in_specs=placed, out_specs=P("tp", "req", None), check_vma=False)
```

```python
import jax
import jax.numpy as jnp
from jax import lax
from jax.experimental import pallas as pl
from jax.experimental.pallas import tpu as pltpu
from jax.sharding import PartitionSpec as P

HD = 128
MESH = pl.DeviceIdType.MESH
F32 = jnp.float32
BF16 = jnp.bfloat16
VMEM_LIMIT = 60 * 1024 * 1024


class Place:
    def __init__(self):
        r, t = lax.axis_index("req"), lax.axis_index("tp")
        self.r, self.t = r, t
        self.core, self.y, self.zh = r % 2, (r // 2) % 4, r // 8
        self.x, self.zl = t // 2, t % 2
        self.mate = {"req": r + 1 - 2 * self.core}
        self.yp = {"req": self.zh * 8 + ((self.y + 1) % 4) * 2 + self.core}
        self.ym = {"req": self.zh * 8 + ((self.y + 3) % 4) * 2 + self.core}
        self.zp = {"req": ((self.zh + 1) % 4) * 8 + self.y * 2 + self.core}
        self.zm = {"req": ((self.zh + 3) % 4) * 8 + self.y * 2 + self.core}
        self.xp = {"tp": ((self.x + 1) % 4) * 2 + self.zl}
        self.xm = {"tp": ((self.x + 3) % 4) * 2 + self.zl}
        self.zz = {"tp": self.x * 2 + 1 - self.zl}


class Wire:
    def __init__(self, ssem, rsem):
        self.ssem, self.rsem, self.n, self.sent = ssem, rsem, 0, []

    def send(self, src, dst, to, into=None):
        k = self.n
        self.n += 1
        copy = pltpu.make_async_remote_copy(
            src_ref=src, dst_ref=dst, send_sem=self.ssem.at[k], recv_sem=self.rsem.at[k],
            device_id=to, device_id_type=MESH)
        copy.start()
        self.sent.append(copy)
        into = dst if into is None else into
        here = pltpu.make_async_remote_copy(
            src_ref=into, dst_ref=into, send_sem=self.ssem.at[k], recv_sem=self.rsem.at[k],
            device_id=to, device_id_type=MESH)
        return here.wait_recv

    def drain(self):
        for copy in self.sent:
            copy.wait_send()


def greet(peers):
    barrier = pltpu.get_barrier_semaphore()
    for peer in peers:
        pl.semaphore_signal(barrier, inc=1, device_id=peer, device_id_type=MESH)
    pl.semaphore_wait(barrier, len(peers))


def merge(streams):
    due = [next(s, None) for s in streams]
    while any(d is not None for d in due):
        i = min((d, k) for k, d in enumerate(due) if d is not None)[1]
        due[i] = next(streams[i], None)


def scatter_ring(wire, at, me, left, right, rooms, mix, final, times):
    rbr, rbl, fr, fl = rooms
    opp, nxt, prv = (me + 2) % 4, (me + 1) % 4, (me + 3) % 4
    w_rbr = wire.send(at(opp, 0), rbr, left)
    w_rbl = wire.send(at(opp, 1), rbl, right)
    w_fr1 = wire.send(at(prv, 1), fr.at[1], left)
    w_fl0 = wire.send(at(nxt, 0), fl.at[0], right)
    yield times[0]
    w_rbr()
    mix(at(prv, 0), rbr)
    w_fr0 = wire.send(at(prv, 0), fr.at[0], left)
    w_rbl()
    mix(at(nxt, 1), rbl)
    w_fl1 = wire.send(at(nxt, 1), fl.at[1], right)
    yield times[1]
    w_fr1()
    w_fl0()
    w_fr0()
    w_fl1()
    for j in range(2):
        final(j, at(me, j), fr.at[j], fl.at[j])


def gather_ring(wire, at, me, left, right, times, got=None):
    opp, nxt, prv = (me + 2) % 4, (me + 1) % 4, (me + 3) % 4
    w_r = wire.send(at(me, None), at(me, None), left, at(nxt, None))
    w_l = wire.send(at(me, None), at(me, None), right, at(prv, None))
    yield times[0]
    w_l()
    w_o0 = wire.send(at(prv, 0), at(prv, 0), right, at(opp, 0))
    if got:
        got(prv)
    w_r()
    w_o1 = wire.send(at(nxt, 1), at(nxt, 1), left, at(opp, 1))
    if got:
        got(nxt)
    yield times[1]
    w_o0()
    w_o1()
    if got:
        got(opp)


def rows_at(ref, base, size):
    def at(k, j):
        if j is None:
            return ref.at[pl.ds(pl.multiple_of(base + k * size, size), size)]
        half = size // 2
        return ref.at[pl.ds(pl.multiple_of(base + k * size + j * half, half), half)]

    return at


def normalize(values, gain):
    values = values.astype(F32)
    center = values - jnp.mean(values, -1, keepdims=True)
    spread = jnp.mean(center * center, -1, keepdims=True)
    return (center * lax.rsqrt(spread + 1e-05) * gain).astype(BF16)


def gather_z_first(wire, p, ref, times):
    own = ref.at[pl.ds(pl.multiple_of(p.t * 32, 32), 32)]
    w_z = wire.send(own, own, p.zz, ref.at[pl.ds(pl.multiple_of(p.x * 64 + (1 - p.zl) * 32, 32), 32)])

    def at(zl):
        def inner(k, j):
            if j is None:
                return ref.at[pl.ds(pl.multiple_of(k * 64 + zl * 32, 32), 32)]
            return ref.at[pl.ds(pl.multiple_of(k * 64 + zl * 32 + j * 16, 16), 16)]
        return inner

    mine = gather_ring(wire, at(p.zl), p.x, p.xm, p.xp, times[1:3])
    next(mine)
    yield times[0]
    w_z()
    other = gather_ring(wire, at(1 - p.zl), p.x, p.xm, p.xp, times[3:5])
    next(other)
    yield times[1]
    next(mine)
    yield times[2]
    next(mine, None)
    yield times[3]
    next(other)
    yield times[4]
    next(other, None)


def gather_x_first(wire, p, ref, times):
    def piece(k, zl):
        return ref.at[pl.ds(pl.multiple_of(k * 64 + zl * 32, 32), 32)]

    def at(k, j):
        if j is None:
            return piece(k, p.zl)
        return ref.at[pl.ds(pl.multiple_of(k * 64 + p.zl * 32 + j * 16, 16), 16)]

    waits = []

    def got(k):
        waits.append(wire.send(piece(k, p.zl), piece(k, p.zl), p.zz, piece(k, 1 - p.zl)))

    ring = gather_ring(wire, at, p.x, p.xm, p.xp, times[0:2], got)
    due = next(ring)
    got(p.x)
    while due is not None:
        yield due
        due = next(ring, None)
    yield times[2]
    for wait in waits:
        wait()


def prefix_half(wire, p, a, kv, own, par, rooms, owner, times):
    held = owner == p.r
    chip = owner // 2 == p.r // 2
    row = owner // 8 == p.zh
    con, done = own.at[a], kv.at[p.core, a]
    con[...] = jnp.where(held, own[a], par[a])
    yrooms, zrooms = rooms
    whose = {}

    def mix(ref, got):
        ref[...] = jnp.where(whose["own"], ref[...], got[...])

    def final(j, ref, fr, fl):
        d = (whose["at"] - whose["me"] + 4) % 4
        far = fr if j == 0 else fl
        near, near_d = (fl, 3) if j == 0 else (fr, 1)
        into = whose["into"](whose["me"], j)
        into[...] = jnp.where(d == 0, ref[...], jnp.where(d == near_d, near[...], far[...]))

    yat = rows_at(con, 0, 512)
    whose.update(own=chip, at=(owner // 2) % 4, me=p.y, into=yat)
    yield from scatter_ring(wire, yat, p.y, p.ym, p.yp, yrooms, mix, final, times[0:2])
    zat, zdone = rows_at(con, p.y * 512, 128), rows_at(done, p.y * 512, 128)
    ydone = rows_at(done, 0, 512)
    whose.update(own=row, at=owner // 8, me=p.zh, into=zdone)
    yield from scatter_ring(wire, zat, p.zh, p.zm, p.zp, zrooms, mix, final, times[2:4])
    yield from gather_ring(wire, zdone, p.zh, p.zm, p.zp, times[4:6])
    theirs = rows_at(kv.at[1 - p.core, a], 0, 512)
    waits = []

    def got(k):
        waits.append(wire.send(ydone(k, None), ydone(k, None), p.mate, theirs(k, None)))

    ring = gather_ring(wire, ydone, p.y, p.ym, p.yp, times[6:8], got)
    due = next(ring)
    got(p.y)
    while due is not None:
        yield due
        due = next(ring, None)
    yield times[8]
    for wait in waits:
        wait()


def attend(qkv, kv, ctx, s, group, length):
    scale = HD ** (-0.5)
    rows = lax.broadcasted_iota(jnp.int32, (256, 256), 0)
    cols = lax.broadcasted_iota(jnp.int32, (256, 256), 1)
    visible = (cols <= rows) & (cols < length)
    nt = (((1,), (1,)), ((), ()))
    for h in range(2):
        lanes = slice(h * HD, (h + 1) * HD)
        q = qkv[0, s, :, lanes]
        pre = lax.dot_general(q, kv[group, 0, :, lanes], nt, preferred_element_type=F32) * scale
        own = lax.dot_general(q, qkv[1, s, :, lanes], nt, preferred_element_type=F32) * scale
        own = jnp.where(visible, own, -jnp.inf)
        top = jnp.maximum(jnp.max(pre, -1, keepdims=True), jnp.max(own, -1, keepdims=True))
        pre = jnp.exp(pre - top)
        own = jnp.exp(own - top)
        total = jnp.sum(pre, -1, keepdims=True) + jnp.sum(own, -1, keepdims=True)
        out = jnp.dot(pre.astype(BF16), kv[group, 1, :, lanes], preferred_element_type=F32)
        out = out + jnp.dot(own.astype(BF16), qkv[2, s, :, lanes], preferred_element_type=F32)
        ctx[s, :, lanes] = (out / total).astype(BF16)


def add(ref, got):
    ref[...] = (ref[...].astype(F32) + got[...].astype(F32)).astype(BF16)


def scatter_z_first(wire, p, part, total, away, zroom, rooms, times):
    order = [(p.x + d) % 4 for d in (2, 3, 1, 0)]

    def rows(k, zl):
        return part.at[pl.ds(pl.multiple_of(k * 64 + zl * 32, 32), 32)]

    def at(k, j):
        return part.at[pl.ds(pl.multiple_of(k * 64 + p.zl * 32 + j * 16, 16), 16)]

    def final(j, ref, fr, fl):
        total[j * 16:(j + 1) * 16] = ref[...].astype(F32) + fr[...].astype(F32) + fl[...].astype(F32)

    waits = [wire.send(rows(k, 1 - p.zl), zroom.at[i], p.zz) for i, k in enumerate(order)]
    yield times[0]
    for i in range(3):
        waits[i]()
        add(rows(order[i], p.zl), zroom.at[i])
    yield from scatter_ring(wire, at, p.x, p.xm, p.xp, rooms, add, final, times[1:3])
    waits[3]()
    total[...] = total[...] + zroom[3].astype(F32)


def scatter_x_first(wire, p, part, total, away, zroom, rooms, times):
    waits = []

    def at(k, j):
        zl = p.zl if j else 1 - p.zl
        return part.at[pl.ds(pl.multiple_of(k * 64 + zl * 32, 32), 32)]

    def final(j, ref, fr, fl):
        here = ref[...].astype(F32) + fr[...].astype(F32) + fl[...].astype(F32)
        if j:
            total[...] = here
        else:
            away[...] = here.astype(BF16)
            waits.append(wire.send(away, zroom, p.zz))

    yield from scatter_ring(wire, at, p.x, p.xm, p.xp, rooms, add, final, times[0:2])
    yield times[2]
    waits[0]()
    total[...] = total[...] + zroom[...].astype(F32)


def gelu(v):
    return 0.5 * v * (1.0 + lax.erf(v * (0.5 ** 0.5)))


def spread(left, w, into):
    @pl.loop(0, 4)
    def _(j):
        lanes = pl.ds(pl.multiple_of(j * 512, 512), 512)
        into[:, lanes] = jnp.dot(left[...], w[:, lanes], preferred_element_type=F32).astype(BF16)


def layer_kernel(owner_ref, group_ref, perm_ref, len_ref, x_ref, gain_ref, gain2_ref, block, w_any, wo_any, wi_any,
                 wd_any, out, xg, own, par, kv, w, qkv, yr0, yf0, yr1, yf1, zr0, zf0, zr1, zf1, ctx, wo, wi, wd,
                 parts, total, hid, ng, inner, away, zra, zrb, xra, xfa, xrb, xfb, ssem, rsem, lsem):
    p = Place()
    copies = [pltpu.make_async_copy(block.at[a], own.at[a], lsem.at[a]) for a in range(2)]
    weights = pltpu.make_async_copy(w_any, w, lsem.at[2])
    for copy in copies:
        copy.start()
    weights.start()
    later = [pltpu.make_async_copy(a, b, lsem.at[3 + i])
             for i, (a, b) in enumerate([(wo_any, wo), (wi_any, wi), (wd_any, wd)])]
    for copy in later:
        copy.start()
    greet([p.mate, p.yp, p.ym, p.zp, p.zm, p.xp, p.xm, p.zz])
    wire = Wire(ssem, rsem)
    w_par = [wire.send(block.at[a], par.at[a], p.mate) for a in range(2)]
    for s in range(2):
        xg[s, pl.ds(pl.multiple_of(p.t * 32, 32), 32)] = normalize(x_ref[s], gain_ref[...])
    owner = owner_ref[p.core]

    def prefix(a, start, times):
        yield start
        copies[a].wait()
        w_par[a]()
        yr, yf, zr, zf = ((yr0, yf0, zr0, zf0), (yr1, yf1, zr1, zf1))[a]
        rooms = ((yr.at[0], yr.at[1], yf.at[0], yf.at[1]), (zr.at[0], zr.at[1], zf.at[0], zf.at[1]))
        yield from prefix_half(wire, p, a, kv, own, par, rooms, owner, times)

    def project(start):
        yield start
        weights.wait()
        for s in (1, 0):
            @pl.loop(0, 3)
            def _(j):
                qkv[j, s] = jnp.dot(xg[s], w[j], preferred_element_type=F32).astype(BF16)
            yield start + 1

    merge([
        gather_z_first(wire, p, xg.at[0], (4, 9, 12, 15, 18)),
        gather_x_first(wire, p, xg.at[1], (5, 8, 20)),
        prefix(0, 2, (8, 12, 15, 18, 21, 24, 29, 33, 40)),
        prefix(1, 5, (15, 20, 24, 26, 29, 31, 38, 42, 46)),
        project(21),
    ])
    requests = [perm_ref[p.r * 2 + s] for s in range(2)]

    def scatter(s, step, times):
        if s == 0:
            rooms = (xra.at[step, 0], xra.at[step, 1], xfa.at[step, 0], xfa.at[step, 1])
            return scatter_z_first(wire, p, parts.at[step, s], total.at[s], None, zra.at[step], rooms, times)
        rooms = (xrb.at[step, 0], xrb.at[step, 1], xfb.at[step, 0], xfb.at[step, 1])
        return scatter_x_first(wire, p, parts.at[step, s], total.at[s], away.at[step], zrb.at[step], rooms, times)

    def slot(s, start, times):
        yield start
        attend(qkv, kv, ctx, s, group_ref[requests[s]], len_ref[requests[s]])
        if s == 0:
            later[0].wait()
        spread(ctx.at[s], wo, parts.at[0, s])
        yield from scatter(s, 0, times[0])
        hid[s] = (x_ref[s].astype(F32) + total[s]).astype(BF16)
        ng[s, pl.ds(pl.multiple_of(p.t * 32, 32), 32)] = normalize(hid[s], gain2_ref[...])
        yield from (gather_x_first if s else gather_z_first)(wire, p, ng.at[s], times[1])
        if s == 0:
            later[1].wait()
            later[2].wait()

        @pl.loop(0, 2)
        def _(i):
            rows = pl.ds(pl.multiple_of(i * 128, 128), 128)
            inner[s, rows] = gelu(jnp.dot(ng[s, rows], wi[...], preferred_element_type=F32)).astype(BF16)

        spread(inner.at[s], wd, parts.at[1, s])
        yield from scatter(s, 1, times[2])
        places = p.t * 32 + lax.broadcasted_iota(jnp.int32, (32, 2048), 0)
        out[s] = jnp.where(places < len_ref[requests[s]], hid[s].astype(F32) + total[s], 0.0).astype(BF16)

    merge([
        slot(0, 0, ((13, 16, 18.5), (23, 28, 31, 33, 35), (49, 52, 54.5))),
        slot(1, 4, ((8.5, 13.5, 17.5), (22, 25, 37), (43, 48, 52.5))),
    ])
    wire.drain()


def on_device(suffix, prefix_store, prefix_owner, prefix_group, request_perm, suffix_len, ln_gain_attn,
              w_qkv, w_out_attn, ln_gain_mlp, w_in, w_down):
    rows = jnp.transpose(suffix, (1, 0, 2))
    block = jnp.transpose(prefix_store[0], (1, 0, 2))
    w3 = jnp.transpose(w_qkv, (1, 0, 2))
    vm = pl.BlockSpec(memory_space=pltpu.VMEM)
    sm = pl.BlockSpec(memory_space=pltpu.SMEM)
    anym = pl.BlockSpec(memory_space=pl.ANY)
    out = pl.pallas_call(
        layer_kernel,
        out_shape=jax.ShapeDtypeStruct((2, 32, 2048), BF16),
        in_specs=[sm, sm, sm, sm, vm, vm, vm, anym, anym, anym, anym, anym],
        out_specs=vm,
        scratch_shapes=[
            pltpu.VMEM((2, 256, 2048), BF16),
            pltpu.VMEM((2, 2048, 256), BF16),
            pltpu.VMEM((2, 2048, 256), BF16),
            pltpu.VMEM((2, 2, 2048, 256), BF16),
            pltpu.VMEM((3, 2048, 256), BF16),
            pltpu.VMEM((3, 2, 256, 256), BF16),
            pltpu.VMEM((2, 256, 256), BF16),
            pltpu.VMEM((2, 2, 256, 256), BF16),
            pltpu.VMEM((2, 256, 256), BF16),
            pltpu.VMEM((2, 2, 256, 256), BF16),
            pltpu.VMEM((2, 64, 256), BF16),
            pltpu.VMEM((2, 2, 64, 256), BF16),
            pltpu.VMEM((2, 64, 256), BF16),
            pltpu.VMEM((2, 2, 64, 256), BF16),
            pltpu.VMEM((2, 256, 256), BF16),
            pltpu.VMEM((256, 2048), BF16),
            pltpu.VMEM((2048, 640), BF16),
            pltpu.VMEM((640, 2048), BF16),
            pltpu.VMEM((2, 2, 256, 2048), BF16),
            pltpu.VMEM((2, 32, 2048), F32),
            pltpu.VMEM((2, 32, 2048), BF16),
            pltpu.VMEM((2, 256, 2048), BF16),
            pltpu.VMEM((2, 256, 640), BF16),
            pltpu.VMEM((2, 32, 2048), BF16),
            pltpu.VMEM((2, 4, 32, 2048), BF16),
            pltpu.VMEM((2, 32, 2048), BF16),
            pltpu.VMEM((2, 2, 16, 2048), BF16),
            pltpu.VMEM((2, 2, 2, 16, 2048), BF16),
            pltpu.VMEM((2, 2, 32, 2048), BF16),
            pltpu.VMEM((2, 2, 2, 32, 2048), BF16),
            pltpu.SemaphoreType.DMA((128,)),
            pltpu.SemaphoreType.DMA((128,)),
            pltpu.SemaphoreType.DMA((6,)),
        ],
        compiler_params=pltpu.CompilerParams(
            collective_id=0, has_side_effects=True, vmem_limit_bytes=VMEM_LIMIT),
        name="decoder_layer",
    )(prefix_owner, prefix_group, request_perm, suffix_len, rows, ln_gain_attn.reshape(1, -1),
      ln_gain_mlp.reshape(1, -1), block, w3, w_out_attn, w_in, w_down)
    return jnp.transpose(out, (1, 0, 2))


def solution(mesh):
    placed = (P("tp", "req", None), P("req", None, None, "tp"), P(), P(), P(), P(), P(),
              P(None, None, "tp"), P("tp", None), P(), P(None, "tp"), P("tp", None))
    return jax.shard_map(
        on_device, mesh=mesh, in_specs=placed, out_specs=P("tp", "req", None), check_vma=False)
```

```python
import jax
import jax.numpy as jnp
from jax import lax
from jax.experimental import pallas as pl
from jax.experimental.pallas import tpu as pltpu
from jax.sharding import PartitionSpec as P

HD = 128
MESH = pl.DeviceIdType.MESH
F32 = jnp.float32
BF16 = jnp.bfloat16
VMEM_LIMIT = 60 * 1024 * 1024


class Place:
    def __init__(self):
        r, t = lax.axis_index("req"), lax.axis_index("tp")
        self.r, self.t = r, t
        self.core, self.y, self.zh = r % 2, (r // 2) % 4, r // 8
        self.x, self.zl = t // 2, t % 2
        self.mate = {"req": r + 1 - 2 * self.core}
        self.yp = {"req": self.zh * 8 + ((self.y + 1) % 4) * 2 + self.core}
        self.ym = {"req": self.zh * 8 + ((self.y + 3) % 4) * 2 + self.core}
        self.zp = {"req": ((self.zh + 1) % 4) * 8 + self.y * 2 + self.core}
        self.zm = {"req": ((self.zh + 3) % 4) * 8 + self.y * 2 + self.core}
        self.xp = {"tp": ((self.x + 1) % 4) * 2 + self.zl}
        self.xm = {"tp": ((self.x + 3) % 4) * 2 + self.zl}
        self.zz = {"tp": self.x * 2 + 1 - self.zl}


class Wire:
    def __init__(self, ssem, rsem):
        self.ssem, self.rsem, self.n, self.sent = ssem, rsem, 0, []

    def send(self, src, dst, to, into=None):
        k = self.n
        self.n += 1
        copy = pltpu.make_async_remote_copy(
            src_ref=src, dst_ref=dst, send_sem=self.ssem.at[k], recv_sem=self.rsem.at[k],
            device_id=to, device_id_type=MESH)
        copy.start()
        self.sent.append(copy)
        into = dst if into is None else into
        here = pltpu.make_async_remote_copy(
            src_ref=into, dst_ref=into, send_sem=self.ssem.at[k], recv_sem=self.rsem.at[k],
            device_id=to, device_id_type=MESH)
        return here.wait_recv

    def drain(self):
        for copy in self.sent:
            copy.wait_send()


def greet(peers):
    barrier = pltpu.get_barrier_semaphore()
    for peer in peers:
        pl.semaphore_signal(barrier, inc=1, device_id=peer, device_id_type=MESH)
    pl.semaphore_wait(barrier, len(peers))


def merge(streams):
    due = [next(s, None) for s in streams]
    while any(d is not None for d in due):
        i = min((d, k) for k, d in enumerate(due) if d is not None)[1]
        due[i] = next(streams[i], None)


def scatter_ring(wire, at, me, left, right, rooms, mix, final, times):
    rbr, rbl, fr, fl = rooms
    opp, nxt, prv = (me + 2) % 4, (me + 1) % 4, (me + 3) % 4
    w_rbr = wire.send(at(opp, 0), rbr, left)
    w_rbl = wire.send(at(opp, 1), rbl, right)
    w_fr1 = wire.send(at(prv, 1), fr.at[1], left)
    w_fl0 = wire.send(at(nxt, 0), fl.at[0], right)
    yield times[0]
    w_rbr()
    mix(at(prv, 0), rbr)
    w_fr0 = wire.send(at(prv, 0), fr.at[0], left)
    w_rbl()
    mix(at(nxt, 1), rbl)
    w_fl1 = wire.send(at(nxt, 1), fl.at[1], right)
    yield times[1]
    w_fr1()
    w_fl0()
    w_fr0()
    w_fl1()
    for j in range(2):
        final(j, at(me, j), fr.at[j], fl.at[j])


def gather_ring(wire, at, me, left, right, times, got=None):
    opp, nxt, prv = (me + 2) % 4, (me + 1) % 4, (me + 3) % 4
    w_r = wire.send(at(me, None), at(me, None), left, at(nxt, None))
    w_l = wire.send(at(me, None), at(me, None), right, at(prv, None))
    yield times[0]
    w_l()
    w_o0 = wire.send(at(prv, 0), at(prv, 0), right, at(opp, 0))
    if got:
        got(prv)
    w_r()
    w_o1 = wire.send(at(nxt, 1), at(nxt, 1), left, at(opp, 1))
    if got:
        got(nxt)
    yield times[1]
    w_o0()
    w_o1()
    if got:
        got(opp)


def rows_at(ref, base, size):
    def at(k, j):
        if j is None:
            return ref.at[pl.ds(pl.multiple_of(base + k * size, size), size)]
        half = size // 2
        return ref.at[pl.ds(pl.multiple_of(base + k * size + j * half, half), half)]

    return at


def normalize(values, gain):
    values = values.astype(F32)
    center = values - jnp.mean(values, -1, keepdims=True)
    spread = jnp.mean(center * center, -1, keepdims=True)
    return (center * lax.rsqrt(spread + 1e-05) * gain).astype(BF16)


def gather_z_first(wire, p, ref, times):
    own = ref.at[pl.ds(pl.multiple_of(p.t * 32, 32), 32)]
    w_z = wire.send(own, own, p.zz, ref.at[pl.ds(pl.multiple_of(p.x * 64 + (1 - p.zl) * 32, 32), 32)])

    def at(zl):
        def inner(k, j):
            if j is None:
                return ref.at[pl.ds(pl.multiple_of(k * 64 + zl * 32, 32), 32)]
            return ref.at[pl.ds(pl.multiple_of(k * 64 + zl * 32 + j * 16, 16), 16)]
        return inner

    mine = gather_ring(wire, at(p.zl), p.x, p.xm, p.xp, times[1:3])
    next(mine)
    yield times[0]
    w_z()
    other = gather_ring(wire, at(1 - p.zl), p.x, p.xm, p.xp, times[3:5])
    next(other)
    yield times[1]
    next(mine)
    yield times[2]
    next(mine, None)
    yield times[3]
    next(other)
    yield times[4]
    next(other, None)


def gather_x_first(wire, p, ref, times):
    def piece(k, zl):
        return ref.at[pl.ds(pl.multiple_of(k * 64 + zl * 32, 32), 32)]

    def at(k, j):
        if j is None:
            return piece(k, p.zl)
        return ref.at[pl.ds(pl.multiple_of(k * 64 + p.zl * 32 + j * 16, 16), 16)]

    waits = []

    def got(k):
        waits.append(wire.send(piece(k, p.zl), piece(k, p.zl), p.zz, piece(k, 1 - p.zl)))

    ring = gather_ring(wire, at, p.x, p.xm, p.xp, times[0:2], got)
    due = next(ring)
    got(p.x)
    while due is not None:
        yield due
        due = next(ring, None)
    yield times[2]
    for wait in waits:
        wait()


def prefix_half(wire, p, a, kv, own, par, rooms, owner, times):
    held = owner == p.r
    chip = owner // 2 == p.r // 2
    row = owner // 8 == p.zh
    con, done = own.at[a], kv[a].at[p.core]
    con[...] = jnp.where(held, own[a], par[a])
    yrooms, zrooms = rooms
    whose = {}

    def mix(ref, got):
        ref[...] = jnp.where(whose["own"], ref[...], got[...])

    def final(j, ref, fr, fl):
        d = (whose["at"] - whose["me"] + 4) % 4
        far = fr if j == 0 else fl
        near, near_d = (fl, 3) if j == 0 else (fr, 1)
        into = whose["into"](whose["me"], j)
        into[...] = jnp.where(d == 0, ref[...], jnp.where(d == near_d, near[...], far[...]))

    yat = rows_at(con, 0, 512)
    whose.update(own=chip, at=(owner // 2) % 4, me=p.y, into=yat)
    yield from scatter_ring(wire, yat, p.y, p.ym, p.yp, yrooms, mix, final, times[0:2])
    zat, zdone = rows_at(con, p.y * 512, 128), rows_at(done, p.y * 512, 128)
    ydone = rows_at(done, 0, 512)
    whose.update(own=row, at=owner // 8, me=p.zh, into=zdone)
    yield from scatter_ring(wire, zat, p.zh, p.zm, p.zp, zrooms, mix, final, times[2:4])
    yield from gather_ring(wire, zdone, p.zh, p.zm, p.zp, times[4:6])
    theirs = rows_at(kv[a].at[1 - p.core], 0, 512)
    waits = []

    def got(k):
        waits.append(wire.send(ydone(k, None), ydone(k, None), p.mate, theirs(k, None)))

    ring = gather_ring(wire, ydone, p.y, p.ym, p.yp, times[6:8], got)
    due = next(ring)
    got(p.y)
    while due is not None:
        yield due
        due = next(ring, None)
    yield times[8]
    for wait in waits:
        wait()


def weigh(qkv, keys, probs, own_probs, total, s, h, group, length):
    scale = HD ** (-0.5)
    rows = lax.broadcasted_iota(jnp.int32, (256, 256), 0)
    cols = lax.broadcasted_iota(jnp.int32, (256, 256), 1)
    visible = (cols <= rows) & (cols < length)
    nt = (((1,), (1,)), ((), ()))
    lanes = slice(h * HD, (h + 1) * HD)
    q = qkv[0, s, :, lanes]
    pre = lax.dot_general(q, keys[group, :, lanes], nt, preferred_element_type=F32) * scale
    own = lax.dot_general(q, qkv[1, s, :, lanes], nt, preferred_element_type=F32) * scale
    own = jnp.where(visible, own, -jnp.inf)
    top = jnp.maximum(jnp.max(pre, -1, keepdims=True), jnp.max(own, -1, keepdims=True))
    pre = jnp.exp(pre - top)
    own = jnp.exp(own - top)
    total[s, h] = jnp.sum(pre, -1, keepdims=True) + jnp.sum(own, -1, keepdims=True)
    probs[s, h] = pre.astype(BF16)
    own_probs[s, h] = own.astype(BF16)


def collect(qkv, values, probs, own_probs, total, ctx, s, group):
    for h in range(2):
        lanes = slice(h * HD, (h + 1) * HD)
        out = jnp.dot(probs[s, h], values[group, :, lanes], preferred_element_type=F32)
        out = out + jnp.dot(own_probs[s, h], qkv[2, s, :, lanes], preferred_element_type=F32)
        ctx[s, :, lanes] = (out / total[s, h]).astype(BF16)


def add(ref, got):
    ref[...] = (ref[...].astype(F32) + got[...].astype(F32)).astype(BF16)


def scatter_z_first(wire, p, part, total, away, zroom, rooms, times):
    order = [(p.x + d) % 4 for d in (2, 3, 1, 0)]

    def rows(k, zl):
        return part.at[pl.ds(pl.multiple_of(k * 64 + zl * 32, 32), 32)]

    def at(k, j):
        return part.at[pl.ds(pl.multiple_of(k * 64 + p.zl * 32 + j * 16, 16), 16)]

    def final(j, ref, fr, fl):
        total[j * 16:(j + 1) * 16] = ref[...].astype(F32) + fr[...].astype(F32) + fl[...].astype(F32)

    waits = [wire.send(rows(k, 1 - p.zl), zroom.at[i], p.zz) for i, k in enumerate(order)]
    yield times[0]
    for i in range(3):
        waits[i]()
        add(rows(order[i], p.zl), zroom.at[i])
    yield from scatter_ring(wire, at, p.x, p.xm, p.xp, rooms, add, final, times[1:3])
    waits[3]()
    total[...] = total[...] + zroom[3].astype(F32)


def scatter_x_first(wire, p, part, total, away, zroom, rooms, times):
    waits = []

    def at(k, j):
        zl = p.zl if j else 1 - p.zl
        return part.at[pl.ds(pl.multiple_of(k * 64 + zl * 32, 32), 32)]

    def final(j, ref, fr, fl):
        here = ref[...].astype(F32) + fr[...].astype(F32) + fl[...].astype(F32)
        if j:
            total[...] = here
        else:
            away[...] = here.astype(BF16)
            waits.append(wire.send(away, zroom, p.zz))

    yield from scatter_ring(wire, at, p.x, p.xm, p.xp, rooms, add, final, times[0:2])
    yield times[2]
    waits[0]()
    total[...] = total[...] + zroom[...].astype(F32)


def gelu(v):
    return 0.5 * v * (1.0 + lax.erf(v * (0.5 ** 0.5)))


def spread(left, w, into):
    @pl.loop(0, 4)
    def _(j):
        lanes = pl.ds(pl.multiple_of(j * 512, 512), 512)
        into[:, lanes] = jnp.dot(left[...], w[:, lanes], preferred_element_type=F32).astype(BF16)


def layer_kernel(owner_ref, group_ref, perm_ref, len_ref, x_ref, gain_ref, gain2_ref, block, w_any, wo_any, wi_any,
                 wd_any, out, xg, own, par, keys, values, w, qkv, yr0, yf0, yr1, yf1, zr0, zf0, zr1, zf1, ctx, wo, wi, wd,
                 parts, total, hid, ng, inner, away, zra, zrb, xra, xfa, xrb, xfb, probs, own_probs, weight,
                 ssem, rsem, lsem):
    p = Place()
    copies = [pltpu.make_async_copy(block.at[a], own.at[a], lsem.at[a]) for a in range(2)]
    weights = pltpu.make_async_copy(w_any, w, lsem.at[2])
    for copy in copies:
        copy.start()
    weights.start()
    later = [pltpu.make_async_copy(a, b, lsem.at[3 + i])
             for i, (a, b) in enumerate([(wo_any, wo), (wi_any, wi), (wd_any, wd)])]
    for copy in later:
        copy.start()
    greet([p.mate, p.yp, p.ym, p.zp, p.zm, p.xp, p.xm, p.zz])
    wire = Wire(ssem, rsem)
    w_par = [wire.send(block.at[a], par.at[a], p.mate) for a in range(2)]
    for s in range(2):
        xg[s, pl.ds(pl.multiple_of(p.t * 32, 32), 32)] = normalize(x_ref[:, s, :], gain_ref[...])
    owner = owner_ref[p.core]

    def prefix(a, start, times):
        yield start
        copies[a].wait()
        w_par[a]()
        yr, yf, zr, zf = ((yr0, yf0, zr0, zf0), (yr1, yf1, zr1, zf1))[a]
        rooms = ((yr.at[0], yr.at[1], yf.at[0], yf.at[1]), (zr.at[0], zr.at[1], zf.at[0], zf.at[1]))
        yield from prefix_half(wire, p, a, (keys, values), own, par, rooms, owner, times)

    def project(start):
        yield start
        weights.wait()
        for s in (1, 0):
            @pl.loop(0, 3)
            def _(j):
                qkv[j, s] = jnp.dot(xg[s], w[j], preferred_element_type=F32).astype(BF16)
            yield start + 1

    requests = [perm_ref[p.r * 2 + s] for s in range(2)]

    def score(times):
        for s in range(2):
            for h in range(2):
                yield times[2 * s + h]
                weigh(qkv, keys, probs, own_probs, weight, s, h, group_ref[requests[s]], len_ref[requests[s]])

    merge([
        gather_z_first(wire, p, xg.at[0], (4, 9, 12, 15, 18)),
        gather_x_first(wire, p, xg.at[1], (5, 8, 20)),
        prefix(0, 2, (8, 12, 15, 18, 21, 24, 29, 33, 40)),
        prefix(1, 5, (15, 20, 24, 26, 29, 31, 38, 42, 46)),
        project(21),
        score((40.5, 41.5, 42.5, 43.5)),
    ])
    def scatter(s, step, times):
        if s == 0:
            rooms = (xra.at[step, 0], xra.at[step, 1], xfa.at[step, 0], xfa.at[step, 1])
            return scatter_z_first(wire, p, parts.at[step, s], total.at[s], None, zra.at[step], rooms, times)
        rooms = (xrb.at[step, 0], xrb.at[step, 1], xfb.at[step, 0], xfb.at[step, 1])
        return scatter_x_first(wire, p, parts.at[step, s], total.at[s], away.at[step], zrb.at[step], rooms, times)

    def slot(s, start, times):
        yield start
        collect(qkv, values, probs, own_probs, weight, ctx, s, group_ref[requests[s]])
        if s == 0:
            later[0].wait()
        spread(ctx.at[s], wo, parts.at[0, s])
        yield from scatter(s, 0, times[0])
        hid[s] = (x_ref[:, s, :].astype(F32) + total[s]).astype(BF16)
        ng[s, pl.ds(pl.multiple_of(p.t * 32, 32), 32)] = normalize(hid[s], gain2_ref[...])
        yield from (gather_x_first if s else gather_z_first)(wire, p, ng.at[s], times[1])
        if s == 0:
            later[1].wait()
            later[2].wait()

        @pl.loop(0, 2)
        def _(i):
            rows = pl.ds(pl.multiple_of(i * 128, 128), 128)
            inner[s, rows] = gelu(jnp.dot(ng[s, rows], wi[...], preferred_element_type=F32)).astype(BF16)

        spread(inner.at[s], wd, parts.at[1, s])
        yield from scatter(s, 1, times[2])
        places = p.t * 32 + lax.broadcasted_iota(jnp.int32, (32, 2048), 0)
        out[s] = jnp.where(places < len_ref[requests[s]], hid[s].astype(F32) + total[s], 0.0).astype(BF16)

    merge([
        slot(0, 0, ((13, 16, 18.5), (23, 28, 31, 33, 35), (49, 52, 54.5))),
        slot(1, 2, ((7, 12, 16.5), (22, 25, 37), (43, 48, 52.5))),
    ])
    wire.drain()


def on_device(suffix, prefix_store, prefix_owner, prefix_group, request_perm, suffix_len, ln_gain_attn,
              w_qkv, w_out_attn, ln_gain_mlp, w_in, w_down):
    block = jnp.transpose(prefix_store[0], (1, 0, 2))
    w3 = jnp.transpose(w_qkv, (1, 0, 2))
    vm = pl.BlockSpec(memory_space=pltpu.VMEM)
    sm = pl.BlockSpec(memory_space=pltpu.SMEM)
    anym = pl.BlockSpec(memory_space=pl.ANY)
    out = pl.pallas_call(
        layer_kernel,
        out_shape=jax.ShapeDtypeStruct((2, 32, 2048), BF16),
        in_specs=[sm, sm, sm, sm, vm, vm, vm, anym, anym, anym, anym, anym],
        out_specs=vm,
        scratch_shapes=[
            pltpu.VMEM((2, 256, 2048), BF16),
            pltpu.VMEM((2, 2048, 256), BF16),
            pltpu.VMEM((2, 2048, 256), BF16),
            pltpu.VMEM((2, 2048, 256), BF16),
            pltpu.VMEM((2, 2048, 256), BF16),
            pltpu.VMEM((3, 2048, 256), BF16),
            pltpu.VMEM((3, 2, 256, 256), BF16),
            pltpu.VMEM((2, 256, 256), BF16),
            pltpu.VMEM((2, 2, 256, 256), BF16),
            pltpu.VMEM((2, 256, 256), BF16),
            pltpu.VMEM((2, 2, 256, 256), BF16),
            pltpu.VMEM((2, 64, 256), BF16),
            pltpu.VMEM((2, 2, 64, 256), BF16),
            pltpu.VMEM((2, 64, 256), BF16),
            pltpu.VMEM((2, 2, 64, 256), BF16),
            pltpu.VMEM((2, 256, 256), BF16),
            pltpu.VMEM((256, 2048), BF16),
            pltpu.VMEM((2048, 640), BF16),
            pltpu.VMEM((640, 2048), BF16),
            pltpu.VMEM((2, 2, 256, 2048), BF16),
            pltpu.VMEM((2, 32, 2048), F32),
            pltpu.VMEM((2, 32, 2048), BF16),
            pltpu.VMEM((2, 256, 2048), BF16),
            pltpu.VMEM((2, 256, 640), BF16),
            pltpu.VMEM((2, 32, 2048), BF16),
            pltpu.VMEM((2, 4, 32, 2048), BF16),
            pltpu.VMEM((2, 32, 2048), BF16),
            pltpu.VMEM((2, 2, 16, 2048), BF16),
            pltpu.VMEM((2, 2, 2, 16, 2048), BF16),
            pltpu.VMEM((2, 2, 32, 2048), BF16),
            pltpu.VMEM((2, 2, 2, 32, 2048), BF16),
            pltpu.VMEM((2, 2, 256, 2048), BF16),
            pltpu.VMEM((2, 2, 256, 256), BF16),
            pltpu.VMEM((2, 2, 256, 1), F32),
            pltpu.SemaphoreType.DMA((128,)),
            pltpu.SemaphoreType.DMA((128,)),
            pltpu.SemaphoreType.DMA((6,)),
        ],
        compiler_params=pltpu.CompilerParams(
            collective_id=0, has_side_effects=True, vmem_limit_bytes=VMEM_LIMIT),
        name="decoder_layer",
    )(prefix_owner, prefix_group, request_perm, suffix_len, suffix, ln_gain_attn.reshape(1, -1),
      ln_gain_mlp.reshape(1, -1), block, w3, w_out_attn, w_in, w_down)
    return jnp.transpose(out, (1, 0, 2))


def solution(mesh):
    placed = (P("tp", "req", None), P("req", None, None, "tp"), P(), P(), P(), P(), P(),
              P(None, None, "tp"), P("tp", None), P(), P(None, "tp"), P("tp", None))
    return jax.shard_map(
        on_device, mesh=mesh, in_specs=placed, out_specs=P("tp", "req", None), check_vma=False)
```

```python
import jax
import jax.numpy as jnp
from jax import lax
from jax.experimental import pallas as pl
from jax.experimental.pallas import tpu as pltpu
from jax.sharding import PartitionSpec as P

HD = 128
MESH = pl.DeviceIdType.MESH
F32 = jnp.float32
BF16 = jnp.bfloat16
VMEM_LIMIT = 60 * 1024 * 1024


class Place:
    def __init__(self):
        r, t = lax.axis_index("req"), lax.axis_index("tp")
        self.r, self.t = r, t
        self.core, self.y, self.zh = r % 2, (r // 2) % 4, r // 8
        self.x, self.zl = t // 2, t % 2
        self.mate = {"req": r + 1 - 2 * self.core}
        self.yp = {"req": self.zh * 8 + ((self.y + 1) % 4) * 2 + self.core}
        self.ym = {"req": self.zh * 8 + ((self.y + 3) % 4) * 2 + self.core}
        self.zp = {"req": ((self.zh + 1) % 4) * 8 + self.y * 2 + self.core}
        self.zm = {"req": ((self.zh + 3) % 4) * 8 + self.y * 2 + self.core}
        self.xp = {"tp": ((self.x + 1) % 4) * 2 + self.zl}
        self.xm = {"tp": ((self.x + 3) % 4) * 2 + self.zl}
        self.zz = {"tp": self.x * 2 + 1 - self.zl}


class Wire:
    def __init__(self, ssem, rsem):
        self.ssem, self.rsem, self.n, self.sent = ssem, rsem, 0, []

    def send(self, src, dst, to, into=None):
        k = self.n
        self.n += 1
        copy = pltpu.make_async_remote_copy(
            src_ref=src, dst_ref=dst, send_sem=self.ssem.at[k], recv_sem=self.rsem.at[k],
            device_id=to, device_id_type=MESH)
        copy.start()
        self.sent.append(copy)
        into = dst if into is None else into
        here = pltpu.make_async_remote_copy(
            src_ref=into, dst_ref=into, send_sem=self.ssem.at[k], recv_sem=self.rsem.at[k],
            device_id=to, device_id_type=MESH)
        return here.wait_recv

    def drain(self):
        for copy in self.sent:
            copy.wait_send()


def greet(peers):
    barrier = pltpu.get_barrier_semaphore()
    for peer in peers:
        pl.semaphore_signal(barrier, inc=1, device_id=peer, device_id_type=MESH)
    pl.semaphore_wait(barrier, len(peers))


def merge(streams):
    due = [next(s, None) for s in streams]
    while any(d is not None for d in due):
        i = min((d, k) for k, d in enumerate(due) if d is not None)[1]
        due[i] = next(streams[i], None)


def scatter_ring(wire, at, me, left, right, rooms, mix, final, times, ready=None):
    rbr, rbl, fr, fl = rooms
    opp, nxt, prv = (me + 2) % 4, (me + 1) % 4, (me + 3) % 4
    ready = ready or (lambda i: None)
    ready(0)
    w_rbr = wire.send(at(opp, 0), rbr, left)
    w_rbl = wire.send(at(opp, 1), rbl, right)
    ready(1)
    w_fr1 = wire.send(at(prv, 1), fr.at[1], left)
    ready(2)
    w_fl0 = wire.send(at(nxt, 0), fl.at[0], right)
    yield times[0]
    w_rbr()
    mix(at(prv, 0), rbr)
    w_fr0 = wire.send(at(prv, 0), fr.at[0], left)
    w_rbl()
    mix(at(nxt, 1), rbl)
    w_fl1 = wire.send(at(nxt, 1), fl.at[1], right)
    ready(3)
    yield times[1]
    w_fr1()
    w_fl0()
    w_fr0()
    w_fl1()
    for j in range(2):
        final(j, at(me, j), fr.at[j], fl.at[j])


def gather_ring(wire, at, me, left, right, times, got=None):
    opp, nxt, prv = (me + 2) % 4, (me + 1) % 4, (me + 3) % 4
    w_r = wire.send(at(me, None), at(me, None), left, at(nxt, None))
    w_l = wire.send(at(me, None), at(me, None), right, at(prv, None))
    yield times[0]
    w_l()
    w_o0 = wire.send(at(prv, 0), at(prv, 0), right, at(opp, 0))
    if got:
        got(prv)
    w_r()
    w_o1 = wire.send(at(nxt, 1), at(nxt, 1), left, at(opp, 1))
    if got:
        got(nxt)
    yield times[1]
    w_o0()
    w_o1()
    if got:
        got(opp)


def rows_at(ref, base, size):
    def at(k, j):
        if j is None:
            return ref.at[pl.ds(pl.multiple_of(base + k * size, size), size)]
        half = size // 2
        return ref.at[pl.ds(pl.multiple_of(base + k * size + j * half, half), half)]

    return at


def normalize(values, gain):
    values = values.astype(F32)
    center = values - jnp.mean(values, -1, keepdims=True)
    spread = jnp.mean(center * center, -1, keepdims=True)
    return (center * lax.rsqrt(spread + 1e-05) * gain).astype(BF16)


def gather_z_first(wire, p, ref, times):
    own = ref.at[pl.ds(pl.multiple_of(p.t * 32, 32), 32)]
    w_z = wire.send(own, own, p.zz, ref.at[pl.ds(pl.multiple_of(p.x * 64 + (1 - p.zl) * 32, 32), 32)])

    def at(zl):
        def inner(k, j):
            if j is None:
                return ref.at[pl.ds(pl.multiple_of(k * 64 + zl * 32, 32), 32)]
            return ref.at[pl.ds(pl.multiple_of(k * 64 + zl * 32 + j * 16, 16), 16)]
        return inner

    mine = gather_ring(wire, at(p.zl), p.x, p.xm, p.xp, times[1:3])
    next(mine)
    yield times[0]
    w_z()
    other = gather_ring(wire, at(1 - p.zl), p.x, p.xm, p.xp, times[3:5])
    next(other)
    yield times[1]
    next(mine)
    yield times[2]
    next(mine, None)
    yield times[3]
    next(other)
    yield times[4]
    next(other, None)


def gather_x_first(wire, p, ref, times):
    def piece(k, zl):
        return ref.at[pl.ds(pl.multiple_of(k * 64 + zl * 32, 32), 32)]

    def at(k, j):
        if j is None:
            return piece(k, p.zl)
        return ref.at[pl.ds(pl.multiple_of(k * 64 + p.zl * 32 + j * 16, 16), 16)]

    waits = []

    def got(k):
        waits.append(wire.send(piece(k, p.zl), piece(k, p.zl), p.zz, piece(k, 1 - p.zl)))

    ring = gather_ring(wire, at, p.x, p.xm, p.xp, times[0:2], got)
    due = next(ring)
    got(p.x)
    while due is not None:
        yield due
        due = next(ring, None)
    yield times[2]
    for wait in waits:
        wait()


def chunk(p, i):
    return pl.ds(pl.multiple_of((p.y + (2, 3, 1, 0)[i]) % 4 * 512, 512), 512)


def prefix_half(wire, p, a, kv, own, par, w_par, rooms, owner, times):
    held = owner == p.r
    chip = owner // 2 == p.r // 2
    row = owner // 8 == p.zh
    con, done = own.at[a], kv[a].at[p.core]
    yrooms, zrooms = rooms
    whose = {}

    def mix(ref, got):
        ref[...] = jnp.where(whose["own"], ref[...], got[...])

    def final(j, ref, fr, fl):
        d = (whose["at"] - whose["me"] + 4) % 4
        far = fr if j == 0 else fl
        near, near_d = (fl, 3) if j == 0 else (fr, 1)
        into = whose["into"](whose["me"], j)
        into[...] = jnp.where(d == 0, ref[...], jnp.where(d == near_d, near[...], far[...]))

    def ready(i):
        w_par[i]()
        rows = chunk(p, i)
        con[rows] = jnp.where(held, con[rows], par[a, rows])

    yat = rows_at(con, 0, 512)
    whose.update(own=chip, at=(owner // 2) % 4, me=p.y, into=yat)
    yield from scatter_ring(wire, yat, p.y, p.ym, p.yp, yrooms, mix, final, times[0:2], ready)
    zat, zdone = rows_at(con, p.y * 512, 128), rows_at(done, p.y * 512, 128)
    ydone = rows_at(done, 0, 512)
    whose.update(own=row, at=owner // 8, me=p.zh, into=zdone)
    yield from scatter_ring(wire, zat, p.zh, p.zm, p.zp, zrooms, mix, final, times[2:4])
    yield from gather_ring(wire, zdone, p.zh, p.zm, p.zp, times[4:6])
    theirs = rows_at(kv[a].at[1 - p.core], 0, 512)
    waits = []

    def got(k):
        waits.append(wire.send(ydone(k, None), ydone(k, None), p.mate, theirs(k, None)))

    ring = gather_ring(wire, ydone, p.y, p.ym, p.yp, times[6:8], got)
    due = next(ring)
    got(p.y)
    while due is not None:
        yield due
        due = next(ring, None)
    yield times[8]
    for wait in waits:
        wait()


def weigh(qkv, keys, probs, own_probs, total, s, h, group, length):
    scale = HD ** (-0.5)
    rows = lax.broadcasted_iota(jnp.int32, (256, 256), 0)
    cols = lax.broadcasted_iota(jnp.int32, (256, 256), 1)
    visible = (cols <= rows) & (cols < length)
    nt = (((1,), (1,)), ((), ()))
    lanes = slice(h * HD, (h + 1) * HD)
    q = qkv[0, s, :, lanes]
    pre = lax.dot_general(q, keys[group, :, lanes], nt, preferred_element_type=F32) * scale
    own = lax.dot_general(q, qkv[1, s, :, lanes], nt, preferred_element_type=F32) * scale
    own = jnp.where(visible, own, -jnp.inf)
    top = jnp.maximum(jnp.max(pre, -1, keepdims=True), jnp.max(own, -1, keepdims=True))
    pre = jnp.exp(pre - top)
    own = jnp.exp(own - top)
    total[s, h] = jnp.sum(pre, -1, keepdims=True) + jnp.sum(own, -1, keepdims=True)
    probs[s, h] = pre.astype(BF16)
    own_probs[s, h] = own.astype(BF16)


def collect(qkv, values, probs, own_probs, total, ctx, s, group):
    for h in range(2):
        lanes = slice(h * HD, (h + 1) * HD)
        out = jnp.dot(probs[s, h], values[group, :, lanes], preferred_element_type=F32)
        out = out + jnp.dot(own_probs[s, h], qkv[2, s, :, lanes], preferred_element_type=F32)
        ctx[s, :, lanes] = (out / total[s, h]).astype(BF16)


def add(ref, got):
    ref[...] = (ref[...].astype(F32) + got[...].astype(F32)).astype(BF16)


def scatter_z_first(wire, p, part, total, away, zroom, rooms, times):
    order = [(p.x + d) % 4 for d in (2, 3, 1, 0)]

    def rows(k, zl):
        return part.at[pl.ds(pl.multiple_of(k * 64 + zl * 32, 32), 32)]

    def at(k, j):
        return part.at[pl.ds(pl.multiple_of(k * 64 + p.zl * 32 + j * 16, 16), 16)]

    def final(j, ref, fr, fl):
        total[j * 16:(j + 1) * 16] = ref[...].astype(F32) + fr[...].astype(F32) + fl[...].astype(F32)

    waits = [wire.send(rows(k, 1 - p.zl), zroom.at[i], p.zz) for i, k in enumerate(order)]
    yield times[0]
    for i in range(3):
        waits[i]()
        add(rows(order[i], p.zl), zroom.at[i])
    yield from scatter_ring(wire, at, p.x, p.xm, p.xp, rooms, add, final, times[1:3])
    waits[3]()
    total[...] = total[...] + zroom[3].astype(F32)


def scatter_x_first(wire, p, part, total, away, zroom, rooms, times):
    waits = []

    def at(k, j):
        zl = p.zl if j else 1 - p.zl
        return part.at[pl.ds(pl.multiple_of(k * 64 + zl * 32, 32), 32)]

    def final(j, ref, fr, fl):
        here = ref[...].astype(F32) + fr[...].astype(F32) + fl[...].astype(F32)
        if j:
            total[...] = here
        else:
            away[...] = here.astype(BF16)
            waits.append(wire.send(away, zroom, p.zz))

    yield from scatter_ring(wire, at, p.x, p.xm, p.xp, rooms, add, final, times[0:2])
    yield times[2]
    waits[0]()
    total[...] = total[...] + zroom[...].astype(F32)


def gelu(v):
    return 0.5 * v * (1.0 + lax.erf(v * (0.5 ** 0.5)))


def spread(left, w, into):
    @pl.loop(0, 4)
    def _(j):
        lanes = pl.ds(pl.multiple_of(j * 512, 512), 512)
        into[:, lanes] = jnp.dot(left[...], w[:, lanes], preferred_element_type=F32).astype(BF16)


def layer_kernel(owner_ref, group_ref, perm_ref, len_ref, x_ref, gain_ref, gain2_ref, block, w_any, wo_any, wi_any,
                 wd_any, out, xg, own, par, keys, values, w, qkv, yr0, yf0, yr1, yf1, zr0, zf0, zr1, zf1, ctx, wo, wi, wd,
                 parts, total, hid, ng, inner, away, zra, zrb, xra, xfa, xrb, xfb, probs, own_probs, weight,
                 ssem, rsem, lsem):
    p = Place()
    copies = [pltpu.make_async_copy(block.at[a], own.at[a], lsem.at[a]) for a in range(2)]
    weights = pltpu.make_async_copy(w_any, w, lsem.at[2])
    for copy in copies:
        copy.start()
    weights.start()
    later = [pltpu.make_async_copy(a, b, lsem.at[3 + i])
             for i, (a, b) in enumerate([(wo_any, wo), (wi_any, wi), (wd_any, wd)])]
    for copy in later:
        copy.start()
    greet([p.mate, p.yp, p.ym, p.zp, p.zm, p.xp, p.xm, p.zz])
    wire = Wire(ssem, rsem)
    w_par = [[wire.send(block.at[a, chunk(p, i)], par.at[a, chunk(p, i)], p.mate) for i in range(4)]
             for a in range(2)]
    for s in range(2):
        xg[s, pl.ds(pl.multiple_of(p.t * 32, 32), 32)] = normalize(x_ref[:, s, :], gain_ref[...])
    owner = owner_ref[p.core]

    def prefix(a, start, times):
        yield start
        copies[a].wait()
        yr, yf, zr, zf = ((yr0, yf0, zr0, zf0), (yr1, yf1, zr1, zf1))[a]
        rooms = ((yr.at[0], yr.at[1], yf.at[0], yf.at[1]), (zr.at[0], zr.at[1], zf.at[0], zf.at[1]))
        yield from prefix_half(wire, p, a, (keys, values), own, par, w_par[a], rooms, owner, times)

    def project(start):
        yield start
        weights.wait()
        for s in (1, 0):
            @pl.loop(0, 3)
            def _(j):
                qkv[j, s] = jnp.dot(xg[s], w[j], preferred_element_type=F32).astype(BF16)
            yield start + 1

    requests = [perm_ref[p.r * 2 + s] for s in range(2)]

    def score(times):
        for s in range(2):
            for h in range(2):
                yield times[2 * s + h]
                weigh(qkv, keys, probs, own_probs, weight, s, h, group_ref[requests[s]], len_ref[requests[s]])

    merge([
        gather_z_first(wire, p, xg.at[0], (4, 9, 12, 15, 18)),
        gather_x_first(wire, p, xg.at[1], (5, 8, 20)),
        prefix(0, 2, (8, 12, 15, 18, 21, 24, 29, 33, 40)),
        prefix(1, 5, (15, 20, 24, 26, 29, 31, 38, 42, 46)),
        project(21),
        score((40.5, 41.5, 42.5, 43.5)),
    ])
    def scatter(s, step, times):
        if s == 0:
            rooms = (xra.at[step, 0], xra.at[step, 1], xfa.at[step, 0], xfa.at[step, 1])
            return scatter_z_first(wire, p, parts.at[step, s], total.at[s], None, zra.at[step], rooms, times)
        rooms = (xrb.at[step, 0], xrb.at[step, 1], xfb.at[step, 0], xfb.at[step, 1])
        return scatter_x_first(wire, p, parts.at[step, s], total.at[s], away.at[step], zrb.at[step], rooms, times)

    def slot(s, start, times):
        yield start
        collect(qkv, values, probs, own_probs, weight, ctx, s, group_ref[requests[s]])
        if s == 0:
            later[0].wait()
        spread(ctx.at[s], wo, parts.at[0, s])
        yield from scatter(s, 0, times[0])
        hid[s] = (x_ref[:, s, :].astype(F32) + total[s]).astype(BF16)
        ng[s, pl.ds(pl.multiple_of(p.t * 32, 32), 32)] = normalize(hid[s], gain2_ref[...])
        yield from (gather_x_first if s else gather_z_first)(wire, p, ng.at[s], times[1])
        if s == 0:
            later[1].wait()
            later[2].wait()

        @pl.loop(0, 2)
        def _(i):
            rows = pl.ds(pl.multiple_of(i * 128, 128), 128)
            inner[s, rows] = gelu(jnp.dot(ng[s, rows], wi[...], preferred_element_type=F32)).astype(BF16)

        spread(inner.at[s], wd, parts.at[1, s])
        yield from scatter(s, 1, times[2])
        places = p.t * 32 + lax.broadcasted_iota(jnp.int32, (32, 2048), 0)
        total[s] = jnp.where(places < len_ref[requests[s]], hid[s].astype(F32) + total[s], 0.0)

    merge([
        slot(0, 0, ((13, 16, 18.5), (23, 28, 31, 33, 35), (49, 52, 54.5))),
        slot(1, 2, ((7, 12, 16.5), (22, 25, 37), (43, 48, 52.5))),
    ])
    out[...] = jnp.stack([total[0], total[1]], axis=1).astype(BF16)
    wire.drain()


def on_device(suffix, prefix_store, prefix_owner, prefix_group, request_perm, suffix_len, ln_gain_attn,
              w_qkv, w_out_attn, ln_gain_mlp, w_in, w_down):
    block = jnp.transpose(prefix_store[0], (1, 0, 2))
    w3 = jnp.transpose(w_qkv, (1, 0, 2))
    vm = pl.BlockSpec(memory_space=pltpu.VMEM)
    sm = pl.BlockSpec(memory_space=pltpu.SMEM)
    anym = pl.BlockSpec(memory_space=pl.ANY)
    out = pl.pallas_call(
        layer_kernel,
        out_shape=jax.ShapeDtypeStruct((32, 2, 2048), BF16),
        in_specs=[sm, sm, sm, sm, vm, vm, vm, anym, anym, anym, anym, anym],
        out_specs=vm,
        scratch_shapes=[
            pltpu.VMEM((2, 256, 2048), BF16),
            pltpu.VMEM((2, 2048, 256), BF16),
            pltpu.VMEM((2, 2048, 256), BF16),
            pltpu.VMEM((2, 2048, 256), BF16),
            pltpu.VMEM((2, 2048, 256), BF16),
            pltpu.VMEM((3, 2048, 256), BF16),
            pltpu.VMEM((3, 2, 256, 256), BF16),
            pltpu.VMEM((2, 256, 256), BF16),
            pltpu.VMEM((2, 2, 256, 256), BF16),
            pltpu.VMEM((2, 256, 256), BF16),
            pltpu.VMEM((2, 2, 256, 256), BF16),
            pltpu.VMEM((2, 64, 256), BF16),
            pltpu.VMEM((2, 2, 64, 256), BF16),
            pltpu.VMEM((2, 64, 256), BF16),
            pltpu.VMEM((2, 2, 64, 256), BF16),
            pltpu.VMEM((2, 256, 256), BF16),
            pltpu.VMEM((256, 2048), BF16),
            pltpu.VMEM((2048, 640), BF16),
            pltpu.VMEM((640, 2048), BF16),
            pltpu.VMEM((2, 2, 256, 2048), BF16),
            pltpu.VMEM((2, 32, 2048), F32),
            pltpu.VMEM((2, 32, 2048), BF16),
            pltpu.VMEM((2, 256, 2048), BF16),
            pltpu.VMEM((2, 256, 640), BF16),
            pltpu.VMEM((2, 32, 2048), BF16),
            pltpu.VMEM((2, 4, 32, 2048), BF16),
            pltpu.VMEM((2, 32, 2048), BF16),
            pltpu.VMEM((2, 2, 16, 2048), BF16),
            pltpu.VMEM((2, 2, 2, 16, 2048), BF16),
            pltpu.VMEM((2, 2, 32, 2048), BF16),
            pltpu.VMEM((2, 2, 2, 32, 2048), BF16),
            pltpu.VMEM((2, 2, 256, 2048), BF16),
            pltpu.VMEM((2, 2, 256, 256), BF16),
            pltpu.VMEM((2, 2, 256, 1), F32),
            pltpu.SemaphoreType.DMA((136,)),
            pltpu.SemaphoreType.DMA((136,)),
            pltpu.SemaphoreType.DMA((6,)),
        ],
        compiler_params=pltpu.CompilerParams(
            collective_id=0, has_side_effects=True, vmem_limit_bytes=VMEM_LIMIT),
        name="decoder_layer",
    )(prefix_owner, prefix_group, request_perm, suffix_len, suffix, ln_gain_attn.reshape(1, -1),
      ln_gain_mlp.reshape(1, -1), block, w3, w_out_attn, w_in, w_down)
    return out


def solution(mesh):
    placed = (P("tp", "req", None), P("req", None, None, "tp"), P(), P(), P(), P(), P(),
              P(None, None, "tp"), P("tp", None), P(), P(None, "tp"), P("tp", None))
    return jax.shard_map(
        on_device, mesh=mesh, in_specs=placed, out_specs=P("tp", "req", None), check_vma=False)
```
